32 devices in a mesh: dp: 16 (over z, x, core), mp: 2 (over y).
Axes of the slice: x: 2, y: 2, z: 4, core: 2. Of those that a mesh axis runs over, the one named last changes fastest.
Arguments:
- tokens: bfloat16 [16384, 1024], P('dp', 'mp'), may hold values from -13 to 13
- pack_class: int32 [16], P('dp'), may hold values from 0 to 2
- ln1_gain: float32 [1024], P('mp'), may hold values from 0.5 to 1.5
- ln1_bias: float32 [1024], P('mp'), may hold values from -1.5 to 1.5
- step_log: float32 [1024], P('mp'), may hold values from -6.9 to -2.3
- lam_log_re: float32 [1024, 32], P('mp'), may hold values from -3 to 0.7
- lam_im: float32 [1024, 32], P('mp'), may hold values from 0 to 100
- p_vec: float32 [2, 1024, 32], P(None, 'mp'), may hold values from -3 to 3
- b_vec: float32 [2, 1024, 32], P(None, 'mp'), may hold values from -5 to 5
- c_vec: float32 [2, 1024, 32], P(None, 'mp'), may hold values from -5 to 5
- skip: float32 [1024], P('mp'), may hold values from -4 to 4
- glu_weight: bfloat16 [1024, 2, 1024], P(None, None, 'mp'), may hold values from -0.1875 to 0.1875
- glu_bias: float32 [2, 1024], P(None, 'mp'), may hold values from -1.5 to 1.5
- ln2_gain: float32 [1024], P('mp'), may hold values from 0.5 to 1.5
- ln2_bias: float32 [1024], P('mp'), may hold values from -1.5 to 1.5
- up_weight: bfloat16 [1024, 4096], P(None, 'mp'), may hold values from -0.1875 to 0.1875
- up_bias: float32 [4096], P('mp'), may hold values from -2.5 to 2.5
- down_weight: bfloat16 [4096, 1024], P('mp'), may hold values from -0.09375 to 0.09375
- down_bias: float32 [1024], P('mp'), may hold values from -1.5 to 1.5
- out_grad: bfloat16 [16384, 1024], P('dp', 'mp'), may hold values from -6 to 6
Outputs:
- result: bfloat16 [16384, 1024], P('dp', 'mp')
- tokens_grad: bfloat16 [16384, 1024], P('dp', 'mp')
- ln1_gain_grad: float32 [1024], P('mp')
- ln1_bias_grad: float32 [1024], P('mp')
- step_log_grad: float32 [1024], P('mp')
- lam_log_re_grad: float32 [1024, 32], P('mp')
- lam_im_grad: float32 [1024, 32], P('mp')
- p_vec_grad: float32 [2, 1024, 32], P(None, 'mp')
- b_vec_grad: float32 [2, 1024, 32], P(None, 'mp')
- c_vec_grad: float32 [2, 1024, 32], P(None, 'mp')
- skip_grad: float32 [1024], P('mp')
- glu_weight_grad: float32 [1024, 2, 1024], P(None, None, 'mp')
- glu_bias_grad: float32 [2, 1024], P(None, 'mp')
- ln2_gain_grad: float32 [1024], P('mp')
- ln2_bias_grad: float32 [1024], P('mp')
- up_weight_grad: float32 [1024, 4096], P(None, 'mp')
- up_bias_grad: float32 [4096], P('mp')
- down_weight_grad: float32 [4096, 1024], P('mp')
- down_bias_grad: float32 [1024], P('mp')
The draws below stay inside these ranges and needn't reach their ends.
All inputs are finite; a program needn't handle non-finite values.
Results may differ from the reference program's by a relative error of at most 0.0064.
Values may be sent and summed in bfloat16 or wider, within the bound.
No kernel may reach another device: no remote copies, remote signals or barrier semaphores. Data moves between devices by JAX's collectives and lax.ppermute only.
A program may use at most 192 MiB of HBM per device.

```python
import math
from functools import partial
import jax
import jax.numpy as jnp
from jax import lax

D = 1024
FF = 4096
PAIRS = 32
PACK = 1024
TOKENS = 16384
N_DP = 16


def draw_tokens(key, part):
    first_key, second_key = jax.random.split(key, 2)
    column = jnp.arange(D).astype(jnp.float32)[None, :] / (D - 1)
    widen = jnp.sqrt(1.0 + 2.0 * column)
    noise = jnp.clip(jax.random.normal(first_key, (TOKENS, D), jnp.float32), -4.0, 4.0)
    factor = jax.random.uniform(second_key, (1, D), jnp.float32, 0.8, 1.25)
    offset = 0.2 * column
    return ((noise * factor + offset) * widen).astype(jnp.bfloat16)


def set_ends(drawn, key, low, top_value):
    spot = [jax.random.randint(jax.random.fold_in(key, axis), (), 0, length) for axis, length in enumerate(drawn.shape)]
    main_axis = drawn.shape.index(max(drawn.shape))
    neighbour = spot[:main_axis] + [(spot[main_axis] + 1) % drawn.shape[main_axis]] + spot[main_axis + 1:]
    return drawn.at[tuple(spot)].set(low).at[tuple(neighbour)].set(top_value)


def levels(stream_key, dims, shards, smallest, largest):
    def one(axis_at, blocks):
        heights = jax.random.uniform(jax.random.fold_in(jax.random.fold_in(stream_key, 6), axis_at), (blocks,), jnp.float32, smallest / len(shards), largest / len(shards))
        return jnp.repeat(jnp.exp(heights), dims[axis_at] // blocks).reshape((-1,) + (1,) * (len(dims) - axis_at - 1))

    level = one(*shards[0])
    for cut in shards[1:]:
        level = level * one(*cut)
    return level


def normal_values(own_key, shape, width, limit, cuts=(), held_as=jnp.bfloat16):
    drawn = jax.random.normal(own_key, shape, jnp.float32) * width
    if len(cuts) > 0:
        drawn = levels(own_key, shape, cuts, -0.22, 0.18) * drawn
    return jnp.clip(drawn, min=-limit, max=limit).astype(held_as)


def setup_inputs(seed: int = 0) -> dict:
    key_list = jax.random.split(jax.random.key(seed), 21)
    return {
        "tokens": draw_tokens(jax.random.fold_in(key_list[20], 71), 0),
        "pack_class": set_ends(jax.random.randint(key_list[1], (N_DP,), 0, 3), jax.random.fold_in(key_list[1], 1), 0, 2).astype(jnp.int32),
        "ln1_gain": jnp.clip(1.0 + 0.1 * jax.random.normal(key_list[2], (D,), jnp.float32), 0.5, 1.5),
        "ln1_bias": normal_values(key_list[3], (D,), 0.3, 1.5, ((0, 2),), jnp.float32),
        "step_log": jnp.clip(-6.9 + 4.6000001430511475 * jax.random.uniform(key_list[4], (D,), jnp.float32) ** levels(key_list[4], (D,), ((0, 2),), -0.2, 0.2), -6.9, -2.3),
        "lam_log_re": jnp.clip(-3.0 + 3.7 * jax.random.uniform(key_list[5], (D, PAIRS), jnp.float32) ** levels(key_list[5], (D, PAIRS), ((0, 2),), -0.2, 0.2), -3.0, 0.7),
        "lam_im": jnp.clip(100.0 * jax.random.uniform(key_list[6], (D, PAIRS), jnp.float32) ** levels(key_list[6], (D, PAIRS), ((0, 2),), -0.2, 0.2), 0.0, 100.0),
        "p_vec": normal_values(key_list[7], (2, D, PAIRS), 0.5, 3.0, ((1, 2),), jnp.float32),
        "b_vec": normal_values(key_list[8], (2, D, PAIRS), 1.0, 5.0, ((1, 2),), jnp.float32),
        "c_vec": normal_values(key_list[9], (2, D, PAIRS), 1.0, 5.0, ((1, 2),), jnp.float32),
        "skip": normal_values(key_list[10], (D,), 1.0, 4.0, ((0, 2),), jnp.float32),
        "glu_weight": normal_values(key_list[11], (D, 2, D), D ** -0.5, 0.1875, ((2, 2),)),
        "glu_bias": normal_values(key_list[12], (2, D), 0.3, 1.5, ((1, 2),), jnp.float32),
        "ln2_gain": jnp.clip(1.0 + 0.1 * jax.random.normal(key_list[13], (D,), jnp.float32), 0.5, 1.5),
        "ln2_bias": normal_values(key_list[14], (D,), 0.3, 1.5, ((0, 2),), jnp.float32),
        "up_weight": normal_values(key_list[15], (D, FF), D ** -0.5, 0.1875, ((1, 2),)),
        "up_bias": normal_values(key_list[16], (FF,), 0.5, 2.5, ((0, 2),), jnp.float32),
        "down_weight": normal_values(key_list[17], (FF, D), FF ** -0.5, 0.09375, ((0, 2),)),
        "down_bias": normal_values(key_list[18], (D,), 0.3, 1.5, ((0, 2),), jnp.float32),
        "out_grad": normal_values(key_list[19], (TOKENS, D), 1.0, 6.0, ((0, 16), (1, 2))),
    }


@jax.custom_vjp
def low(v):
    return lax.optimization_barrier(v.astype(jnp.bfloat16)).astype(jnp.float32)

@jax.custom_vjp
def low_back(v):
    return v

def low_keep(v):
    return (low(v), None)

def low_pass(kept, grad):
    return (grad,)

def back_keep(v):
    return (v, None)

def back_low(kept, grad):
    return (low(grad),)
low.defvjp(low_keep, low_pass)
low_back.defvjp(back_keep, back_low)
epsilon = 1e-05
highest = lax.Precision.HIGHEST

def complex_product(left_real, left_imag, right_real, right_imag):
    return (left_real * right_real - left_imag * right_imag, left_real * right_imag + left_imag * right_real)

def kernel_response(step_now, lam_log_re, lam_im, p_vecs, b_vecs, c_vecs, freq_real, freq_imag):
    cross_cb = complex_product(c_vecs[:, 0], c_vecs[:, 1], b_vecs[:, 0], b_vecs[:, 1])
    cross_cp = complex_product(c_vecs[:, 0], c_vecs[:, 1], p_vecs[:, 0], p_vecs[:, 1])
    cross_pb = complex_product(p_vecs[:, 0], -p_vecs[:, 1], b_vecs[:, 0], b_vecs[:, 1])
    power_pp = p_vecs[:, 0] * p_vecs[:, 0] + p_vecs[:, 1] * p_vecs[:, 1]
    stacked = (-jnp.exp(lam_log_re), lam_im, cross_cb[0], cross_cb[1], cross_cp[0], cross_cp[1], cross_pb[0], cross_pb[1], power_pp, jnp.zeros_like(power_pp))
    stacked = tuple((jnp.transpose(entry) for entry in stacked))
    shape_out = (step_now.shape[0], freq_real.shape[1])
    start_sums = tuple((jnp.zeros(shape_out, jnp.float32) for counter in range(8)))

    def add_state(totals, entry):
        columns = [column_item[:, None] for column_item in entry]
        updated = list(totals)
        for parity in (1.0, -1.0):
            decay_real = step_now * columns[0]
            decay_imag = parity * step_now * columns[1]
            divisor_real = 2.0 * (1.0 - freq_real) - (decay_real * (1.0 + freq_real) - decay_imag * freq_imag)
            divisor_imag = -2.0 * freq_imag - (decay_real * freq_imag + decay_imag * (1.0 + freq_real))
            magnitude = divisor_real * divisor_real + divisor_imag * divisor_imag
            resolvent_real = step_now * divisor_real / magnitude
            resolvent_imag = -step_now * divisor_imag / magnitude
            for position in range(4):
                term_real, term_imag = complex_product(columns[2 + 2 * position], parity * columns[3 + 2 * position], resolvent_real, resolvent_imag)
                updated[2 * position] = updated[2 * position] + term_real
                updated[2 * position + 1] = updated[2 * position + 1] + term_imag
        return (tuple(updated), None)
    sums, unused = lax.scan(add_state, start_sums, stacked)
    shifted_real = 1.0 + freq_real
    shifted_imag = freq_imag
    cross_both = complex_product(sums[2], sums[3], sums[4], sums[5])
    numerator = complex_product(cross_both[0], cross_both[1], shifted_real, shifted_imag)
    guard = complex_product(sums[6], sums[7], shifted_real, shifted_imag)
    guard_real = 1.0 + guard[0]
    guard_imag = guard[1]
    guard_size = guard_real * guard_real + guard_imag * guard_imag
    ratio_real = (numerator[0] * guard_real + numerator[1] * guard_imag) / guard_size
    ratio_imag = (numerator[1] * guard_real - numerator[0] * guard_imag) / guard_size
    return (2.0 * (sums[0] - ratio_real), 2.0 * (sums[1] - ratio_imag))

def kernel_taps(span_size, step_log, lam_log_re, lam_im, p_vec, b_vec, c_vec):
    width_all = step_log.shape[0]
    block_size = min(width_all, 64)
    block_count = width_all // block_size
    index = jnp.arange(span_size, dtype=jnp.int32)
    phase = index.astype(jnp.float32)[None, :] * (2.0 * math.pi / span_size)
    freq_real = jnp.cos(phase)
    freq_imag = -jnp.sin(phase)

    def one_block(block_items):
        step_block, lam_real_block, lam_imag_block, p_block, b_block, c_block = block_items
        khat_real, khat_imag = kernel_response(jnp.exp(step_block)[:, None], lam_real_block, lam_imag_block, p_block, b_block, c_block, freq_real, freq_imag)
        return jnp.real(jnp.fft.ifft(lax.complex(khat_real, khat_imag), axis=-1))
    block_items = (step_log.reshape(block_count, block_size), lam_log_re.reshape(block_count, block_size, -1), lam_im.reshape(block_count, block_size, -1), jnp.transpose(p_vec, (1, 0, 2)).reshape(block_count, block_size, 2, -1), jnp.transpose(b_vec, (1, 0, 2)).reshape(block_count, block_size, 2, -1), jnp.transpose(c_vec, (1, 0, 2)).reshape(block_count, block_size, 2, -1))
    return lax.map(jax.checkpoint(one_block), block_items).reshape(width_all, span_size)

def s4_mixer(normed, ssm_params, span_size):
    step_log, lam_log_re, lam_im, p_vec, b_vec, c_vec, skip = ssm_params
    row_count, width_all = normed.shape
    taps = kernel_taps(span_size, step_log, lam_log_re, lam_im, p_vec, b_vec, c_vec)
    seq_count = row_count // span_size
    sequences = normed.reshape(seq_count, span_size, width_all)
    spec_in = jnp.fft.rfft(sequences, n=2 * span_size, axis=1)
    spec_taps = jnp.fft.rfft(jnp.transpose(taps), n=2 * span_size, axis=0)
    mixed = jnp.fft.irfft(spec_in * spec_taps[None], n=2 * span_size, axis=1)[:, :span_size]
    return jax.nn.gelu(mixed.reshape(row_count, width_all) + skip * normed, approximate=False)

def layer_norm(values, gain, shift_bias):
    mean_row = lax.optimization_barrier(jnp.mean(values, axis=-1, keepdims=True))
    centred = values - mean_row
    var_row = lax.optimization_barrier(jnp.mean(centred * centred, axis=-1, keepdims=True))
    return centred * lax.rsqrt(var_row + epsilon) * gain + shift_bias

def group_forward(group_rows, class_index, weights):
    ln1_gain, ln1_bias, step_log, lam_log_re, lam_im, p_vec, b_vec, c_vec, skip, glu_weight, glu_bias, ln2_gain, ln2_bias, up_weight, up_bias, down_weight, down_bias = weights
    row_count = group_rows.shape[0]
    normed1 = layer_norm(group_rows, ln1_gain, ln1_bias)
    ssm_params = (step_log, lam_log_re, lam_im, p_vec, b_vec, c_vec, skip)
    branches = [partial(s4_mixer, span_size=row_count >> shift_bits) for shift_bits in (0, 2, 3)]
    act = low(lax.switch(class_index, branches, normed1, ssm_params))
    proj = low_back(jnp.einsum('pd,dge->pge', act, glu_weight, precision=highest) + glu_bias)
    residual_mid = group_rows + proj[:, 0] * jax.nn.sigmoid(proj[:, 1])
    normed2 = low(layer_norm(residual_mid, ln2_gain, ln2_bias))
    pre_act = low_back(jnp.dot(normed2, up_weight, precision=highest) + up_bias)
    hidden = low(jax.nn.gelu(pre_act, approximate=False))
    return jnp.dot(hidden, down_weight, precision=highest) + down_bias + residual_mid

def reference(tokens, pack_class, ln1_gain, ln1_bias, step_log, lam_log_re, lam_im, p_vec, b_vec, c_vec, skip, glu_weight, glu_bias, ln2_gain, ln2_bias, up_weight, up_bias, down_weight, down_bias, out_grad):
    weights = tuple((entry.astype(jnp.float32) for entry in (ln1_gain, ln1_bias, step_log, lam_log_re, lam_im, p_vec, b_vec, c_vec, skip, glu_weight, glu_bias, ln2_gain, ln2_bias, up_weight, up_bias, down_weight, down_bias)))
    inputs = tokens.astype(jnp.float32)

    def forward(all_rows, all_weights):
        groups = all_rows.reshape(N_DP, PACK, D)

        def one_group(carry, group_items):
            return (carry, jax.checkpoint(group_forward)(group_items[0], group_items[1], all_weights))
        carry_out, outputs = lax.scan(one_group, jnp.zeros((), jnp.float32), (groups, pack_class))
        return outputs.reshape(TOKENS, D)
    output, pullback = jax.vjp(forward, inputs, weights)
    input_grad, grads = pullback(out_grad.astype(jnp.float32))
    return (output.astype(jnp.bfloat16), input_grad.astype(jnp.bfloat16), grads[0], grads[1], grads[2], grads[3], grads[4], grads[5], grads[6], grads[7], grads[8], grads[9], grads[10], grads[11], grads[12], grads[13], grads[14], grads[15], grads[16])
```

```python
import math

import jax
import jax.numpy as jnp
import numpy as np
from jax import lax
from jax.experimental import pallas as pl
from jax.experimental.pallas import tpu as pltpu
from jax.sharding import PartitionSpec as P

epsilon = 1e-05
highest = lax.Precision.HIGHEST
low = jnp.bfloat16
wide = jnp.float32


def split_table(values):
    high = values.astype(low)
    return (high, (values - high.astype(np.float64)).astype(low))


def transform_tables(row_count):
    tables = []
    for span in (row_count, row_count // 4, row_count // 8):
        order = np.arange(span)
        phase = (np.outer(order, order) % (2 * span)) * (math.pi / span)
        real_rows = np.cos(phase)
        imag_rows = -np.sin(phase)
        imag_rows[0] = 1.0 - 2.0 * (order % 2)
        count = row_count // span
        for copies in (np.eye(count), np.ones((count, count))):
            tables.append(np.concatenate([np.kron(copies, real_rows), np.kron(copies, imag_rows)], axis=0))
    sequences = np.stack([tables[0], tables[2], tables[4]])
    return split_table(np.stack(tables[1:])) + split_table(sequences.transpose(0, 2, 1)) + (sequences.astype(np.float32),)


def response_table(row_count):
    half = row_count // 2
    position = np.arange(row_count)
    phase = (np.outer(np.arange(half), position) % row_count) * (2.0 * math.pi / row_count)
    real_rows = 2.0 * np.cos(phase)
    imag_rows = -2.0 * np.sin(phase)
    real_rows[0] = 1.0
    imag_rows[0] = 1.0 - 2.0 * (position % 2)
    return (np.concatenate([real_rows, imag_rows], axis=0) / row_count).astype(np.float32)


def complex_product(left, right):
    return (left[0] * right[0] - left[1] * right[1], left[0] * right[1] + left[1] * right[0])


def channel_coefficients(step_log, lam_log_re, lam_im, p_vec, b_vec, c_vec):
    step = jnp.exp(step_log)[:, None]
    decay = step * jnp.exp(lam_log_re)
    turn = step * lam_im
    weights = (
        complex_product(c_vec, b_vec),
        complex_product(c_vec, p_vec),
        complex_product((p_vec[0], -p_vec[1]), b_vec),
        (p_vec[0] * p_vec[0] + p_vec[1] * p_vec[1], jnp.zeros_like(decay)),
    )
    flats = [2.0 * (real * decay - imag * turn) for real, imag in weights]
    slopes = [4.0 * real for real, _ in weights]
    last = step * jnp.sum(weights[0][0], axis=1, keepdims=True)
    return (step, last, decay, decay * decay + turn * turn, flats, slopes)


def half_angles(row_count):
    angle = np.arange(row_count // 2) * (math.pi / row_count)
    return (jnp.asarray(np.cos(angle), wide), jnp.asarray(np.sin(angle), wide))


def channel_sums(row_count, decay, squares, flats, slopes):
    cos_half, sin_half = half_angles(row_count)
    bottom_real = squares[:, :, None] * (cos_half * cos_half) - 4.0 * sin_half * sin_half
    bottom_imag = decay[:, :, None] * (4.0 * sin_half * cos_half)
    size = 1.0 / (bottom_real * bottom_real + bottom_imag * bottom_imag)
    part_real = bottom_real * size
    part_imag = -bottom_imag * size
    sums = []
    for flat, slope in zip(flats, slopes):
        flat, slope = flat[:, :, None], slope[:, :, None]
        sums.append(
            (
                cos_half * jnp.sum(flat * part_real, axis=1) - sin_half * jnp.sum(slope * part_imag, axis=1),
                cos_half * jnp.sum(flat * part_imag, axis=1) + sin_half * jnp.sum(slope * part_real, axis=1),
            )
        )
    return sums


def channel_response(row_count, step, last, sums):
    half = row_count // 2
    cos_half, sin_half = half_angles(row_count)
    scale = step * cos_half
    guard_real = 1.0 + scale * sums[3][0]
    guard_imag = scale * sums[3][1]
    guard_size = scale / (guard_real * guard_real + guard_imag * guard_imag)
    cross = complex_product(sums[1], sums[2])
    inner_real = sums[0][0] - (cross[0] * guard_real + cross[1] * guard_imag) * guard_size
    inner_imag = sums[0][1] - (cross[1] * guard_real - cross[0] * guard_imag) * guard_size
    khat_real = step * (cos_half * inner_real - sin_half * inner_imag)
    khat_imag = step * (cos_half * inner_imag + sin_half * inner_real)
    first_slot = jnp.arange(half) == 0
    return jnp.concatenate([khat_real, jnp.where(first_slot, last, khat_imag)], axis=1)


def split(values):
    high = values.astype(low)
    return (high, (values - high.astype(wide)).astype(low))


def split_dot(left, right, contract=(((1,), (0,)), ((), ()))):
    total = None
    for left_part, right_part in ((0, 0), (0, 1), (1, 0)):
        if left_part < len(left) and right_part < len(right):
            term = lax.dot_general(left[left_part], right[right_part], contract, preferred_element_type=wide)
            total = term if total is None else total + term
    return total


def pair_product(left, right, first_rows, conjugate):
    sign = -1.0 if conjugate else 1.0
    plain_imag = left[1] * right[1]
    real = left[0] * right[0] - jnp.where(first_rows, 0.0, sign * plain_imag)
    imag = jnp.where(first_rows, plain_imag, left[1] * right[0] + sign * left[0] * right[1])
    weight = jnp.where(first_rows, 0.5, 1.0)
    return (real * weight, imag * weight)


def first_mask(block, span):
    rows = lax.broadcasted_iota(jnp.int32, (block, 1), 0) + pl.program_id(0) * block
    return (rows & (span - 1)) == 0


def kernel_params():
    return pltpu.CompilerParams(vmem_limit_bytes=56 << 20)


def convolve(choice, tables, turned, input_spectrum, taps):
    double, width = input_spectrum.shape
    length = double // 2
    block = length // 4

    def kernel(
        choice_ref, real_high, real_rest, imag_high, imag_rest, turn_real_high, turn_real_rest, turn_imag_high,
        turn_imag_rest, input_real, input_imag, taps_ref, taps_real, taps_imag, out_ref,
    ):
        over_columns = (((1,), (1,)), ((), ()))
        taps_now = (taps_ref[...],)
        response = (
            split_dot((real_high[0], real_rest[0]), taps_now, over_columns),
            split_dot((imag_high[0], imag_rest[0]), taps_now, over_columns),
        )
        taps_real[...], taps_imag[...] = response
        product = pair_product((input_real[...], input_imag[...]), response, first_mask(block, choice_ref[2]), False)
        update = split_dot((turn_real_high[0], turn_real_rest[0]), split(product[0]))
        update = update + split_dot((turn_imag_high[0], turn_imag_rest[0]), split(product[1]))

        @pl.when(pl.program_id(0) == 0)
        def _():
            out_ref[...] = update

        @pl.when(pl.program_id(0) != 0)
        def _():
            out_ref[...] = out_ref[...] + update

    def table_spec(shift):
        return pl.BlockSpec((1, block, length), lambda at, choice_ref: (choice_ref[1], at + shift, 0))

    def turned_spec(shift):
        return pl.BlockSpec((1, length, block), lambda at, choice_ref: (choice_ref[3], 0, at + shift))

    def rows_spec(shift):
        return pl.BlockSpec((block, width), lambda at, choice_ref: (at + shift, 0))

    whole_spec = pl.BlockSpec((width, length), lambda at, choice_ref: (0, 0))
    result = jax.ShapeDtypeStruct((length, width), wide)
    return pl.pallas_call(
        kernel,
        out_shape=(result, result, result),
        grid_spec=pltpu.PrefetchScalarGridSpec(
            num_scalar_prefetch=1,
            grid=(4,),
            in_specs=[table_spec(0)] * 2
            + [table_spec(4)] * 2
            + [turned_spec(0)] * 2
            + [turned_spec(4)] * 2
            + [rows_spec(0), rows_spec(4), whole_spec],
            out_specs=[rows_spec(0), rows_spec(0), pl.BlockSpec((length, width), lambda at, choice_ref: (0, 0))],
        ),
        cost_estimate=pl.CostEstimate(
            flops=20 * length * length * width, transcendentals=0, bytes_accessed=20 * length * length
        ),
        compiler_params=kernel_params(),
        name="convolve",
    )(choice, *tables, *tables, *turned, *turned, input_spectrum, input_spectrum, taps)


def correlate_taps(choice, tables, grad_spectrum, input_spectrum):
    double, width = grad_spectrum.shape
    length = double // 2
    block = length // 4

    def kernel(
        choice_ref, taps_real_high, taps_real_rest, taps_imag_high, taps_imag_rest, grad_real, grad_imag, input_real,
        input_imag, out_ref,
    ):
        product = pair_product(
            (grad_real[...], grad_imag[...]), (input_real[...], input_imag[...]), first_mask(block, choice_ref[2]), True
        )
        update = split_dot(split(product[0].T), (taps_real_high[0], taps_real_rest[0]))
        update = update + split_dot(split(product[1].T), (taps_imag_high[0], taps_imag_rest[0]))

        @pl.when(pl.program_id(0) == 0)
        def _():
            out_ref[...] = update

        @pl.when(pl.program_id(0) != 0)
        def _():
            out_ref[...] = out_ref[...] + update

    def table_spec(shift):
        return pl.BlockSpec((1, block, length), lambda at, choice_ref: (choice_ref[1], at + shift, 0))

    def rows_spec(shift):
        return pl.BlockSpec((block, width), lambda at, choice_ref: (at + shift, 0))

    return pl.pallas_call(
        kernel,
        out_shape=jax.ShapeDtypeStruct((width, length), wide),
        grid_spec=pltpu.PrefetchScalarGridSpec(
            num_scalar_prefetch=1,
            grid=(4,),
            in_specs=[table_spec(0)] * 2 + [table_spec(4)] * 2 + [rows_spec(0), rows_spec(4)] * 2,
            out_specs=pl.BlockSpec((width, length), lambda at, choice_ref: (0, 0)),
        ),
        cost_estimate=pl.CostEstimate(
            flops=12 * length * length * width, transcendentals=0, bytes_accessed=12 * length * length
        ),
        compiler_params=kernel_params(),
        name="correlate_taps",
    )(choice, *tables, *tables, grad_spectrum, grad_spectrum, input_spectrum, input_spectrum)


def correlate_rows(choice, turned, grad_spectrum, taps_spectrum):
    length, width = taps_spectrum[0].shape
    block = length // 4

    def kernel(
        choice_ref, turn_real, turn_imag, grad_real, grad_imag, taps_real,
        taps_imag, out_ref,
    ):
        product = pair_product(
            (grad_real[...], grad_imag[...]), (taps_real[...], taps_imag[...]), first_mask(block, choice_ref[2]), True
        )
        update = split_dot((turn_real[0],), (product[0].astype(low),))
        update = update + split_dot((turn_imag[0],), (product[1].astype(low),))

        @pl.when(pl.program_id(0) == 0)
        def _():
            out_ref[...] = update

        @pl.when(pl.program_id(0) != 0)
        def _():
            out_ref[...] = out_ref[...] + update

    def turned_spec(shift):
        return pl.BlockSpec((1, length, block), lambda at, choice_ref: (choice_ref[3], 0, at + shift))

    def rows_spec(shift):
        return pl.BlockSpec((block, width), lambda at, choice_ref: (at + shift, 0))

    return pl.pallas_call(
        kernel,
        out_shape=jax.ShapeDtypeStruct((length, width), wide),
        grid_spec=pltpu.PrefetchScalarGridSpec(
            num_scalar_prefetch=1,
            grid=(4,),
            in_specs=[turned_spec(0), turned_spec(4)] + [rows_spec(0), rows_spec(4), rows_spec(0), rows_spec(0)],
            out_specs=pl.BlockSpec((length, width), lambda at, choice_ref: (0, 0)),
        ),
        cost_estimate=pl.CostEstimate(
            flops=4 * length * length * width, transcendentals=0, bytes_accessed=12 * length * length
        ),
        compiler_params=kernel_params(),
        name="correlate_rows",
    )(choice, turned[0], turned[0], grad_spectrum, grad_spectrum, *taps_spectrum)


def gelu_pair(values):
    normal_cdf = 0.5 + 0.5 * lax.erf(values * math.sqrt(0.5))
    density = jnp.exp(-0.5 * values * values) * (1.0 / math.sqrt(2.0 * math.pi))
    return (values * normal_cdf, normal_cdf + values * density)


def swap_pairs(count, bit):
    return [(place, place ^ bit) for place in range(count)]


def dp_gather(shard, dp):
    if dp & (dp - 1):
        return lax.all_gather(shard, "dp", axis=0, tiled=True)
    place = lax.axis_index("dp")
    held = shard[None]
    bits = [1 << turn for turn in reversed(range(dp.bit_length() - 1))]
    shape = shard.shape
    held = shard
    for count, bit in enumerate(bits):
        other = lax.ppermute(held, "dp", swap_pairs(dp, bit))
        is_low = (place & bit) == 0
        held = jnp.where(is_low, jnp.stack([held, other], axis=count), jnp.stack([other, held], axis=count))
    return held.reshape((dp * shape[0],) + shape[1:])


def dp_scatter_sum(values, dp, others):
    if dp & (dp - 1):
        return (lax.psum_scatter(values, "dp", scatter_dimension=0, tiled=True), others)
    place = lax.axis_index("dp")
    bits = [1 << turn for turn in range(dp.bit_length() - 1)]
    held = values.reshape((2,) * len(bits) + (values.shape[0] // dp,) + values.shape[1:])
    for count, bit in enumerate(bits):
        axis = len(bits) - 1 - count
        is_low = (place & bit) == 0
        zero = lax.index_in_dim(held, 0, axis, keepdims=False)
        one = lax.index_in_dim(held, 1, axis, keepdims=False)
        sent = jnp.where(is_low, one, zero).astype(low if count in (1, 2) else wide)
        kept = jnp.where(is_low, zero, one)
        held = kept + lax.ppermute(sent, "dp", swap_pairs(dp, bit)).astype(wide)
        if count == 2:
            held, others = lax.optimization_barrier((held, others))
    return (held, others)


class WeightSum:
    def __init__(self, product, dp, dp_place, far_first):
        self.product = product
        self.dp = dp
        self.dp_place = dp_place
        far = [1 << turn for turn in range(1, dp.bit_length() - 1)]
        self.bits = far[1:] + far[:1] if far_first else far
        self.stage = 0
        self.side = dp_place & 1
        self.first = product(1 - self.side).astype(low)
        self.pending = self.swap(self.first, 1)

    def swap(self, values, bit):
        return lax.ppermute(values, "dp", swap_pairs(self.dp, bit))

    def join(self):
        if self.stage == 0:
            return self.product(self.side) + self.pending.astype(wide)
        return self.kept + self.pending.astype(wide)

    def step(self):
        held = self.join()
        if self.stage == len(self.bits):
            self.share = held.astype(low)
            self.pending = None
            return self.share
        bit = self.bits[self.stage]
        rows = held.shape[0] // 2
        side = jnp.where((self.dp_place & bit) == 0, 0, 1)
        self.kept = lax.dynamic_slice_in_dim(held, side * rows, rows, 0)
        sent = lax.dynamic_slice_in_dim(held, (1 - side) * rows, rows, 0).astype(low)
        self.pending = self.swap(sent, bit)
        self.stage += 1
        return sent

    def block_owner(self, code):
        place = 0
        for turn, bit in enumerate(self.bits[::-1] + [1]):
            place = place + ((code >> turn) & 1) * bit
        return place

    def finish(self):
        while self.pending is not None:
            self.step()
        return self.share


def gather_shares(shares, dp):
    width = math.gcd(*[share.shape[1] for share in shares])
    pieces = []
    places = []
    start = 0
    for share in shares:
        offsets = []
        for column in range(0, share.shape[1], width):
            pieces.append(share[:, column : column + width])
            offsets.append(start)
            start += share.shape[0]
        places.append((share.shape[0], tuple(offsets)))
    block = math.gcd(*[rows for rows, _ in places])
    return lax.all_gather(jnp.concatenate(pieces, axis=0), "dp", axis=0, tiled=True), start, block, places


def response_rows(row_count):
    half = row_count // 2
    angle = np.arange(half) * (math.pi / row_count)
    cosine, sine = np.cos(angle), np.sin(angle)
    rows = [cosine * cosine, 4.0 * sine * sine, 4.0 * sine * cosine, cosine, sine]
    return np.stack(rows + [np.zeros(half)] * 3).astype(np.float32)


def taps_kernel(row_count, share, dp_place, response, step_log, lam_log_re, lam_im, p_vec, b_vec, c_vec):
    half = row_count // 2
    pairs = lam_log_re.shape[1]
    block = math.gcd(share, 8)
    lanes = math.gcd(half, 256)

    wide_block = math.gcd(step_log.shape[0], 128)

    def kernel(
        place_ref, rows_ref, high_ref, rest_ref, step_row, decay_row, turn_row, p_row, b_row, c_row, out_ref, khat_ref,
        step_ref, decay_ref, turn_ref, p_ref, b_ref, c_ref,
    ):
        first = place_ref[0] * share
        inside = lax.rem(first, wide_block)
        near = pl.ds(pl.multiple_of(first - inside, wide_block), wide_block)
        step_ref[...] = jnp.broadcast_to(step_row[:, near], (8, wide_block)).T
        decay_ref[...] = decay_row[:, near].T
        turn_ref[...] = turn_row[:, near].T
        for row, ref in ((p_row, p_ref), (b_row, b_ref), (c_row, c_ref)):
            for side in range(2):
                ref[side] = row[side, :, near].T

        def one_block(at, _):
            where = pl.ds(inside + at * block, block)
            step = jnp.exp(step_ref[where, :][:, :1])
            decay = step * jnp.exp(decay_ref[where, :])
            turn = step * turn_ref[where, :]
            squares = decay * decay + turn * turn
            p_now, b_now, c_now = ((ref[0, where, :], ref[1, where, :]) for ref in (p_ref, b_ref, c_ref))
            weights = (
                complex_product(c_now, b_now),
                complex_product(c_now, p_now),
                complex_product((p_now[0], -p_now[1]), b_now),
                (p_now[0] * p_now[0] + p_now[1] * p_now[1], None),
            )
            flats = [
                2.0 * (pair[0] * decay - pair[1] * turn) if pair[1] is not None else 2.0 * pair[0] * decay
                for pair in weights
            ]
            slopes = [4.0 * pair[0] for pair in weights]
            last = step * jnp.sum(weights[0][0], axis=1, keepdims=True)
            for start in range(0, half, lanes):
                chosen = slice(start, start + lanes)
                cosine_square, sine_square, cross, cosine, sine = (rows_ref[row : row + 1, chosen] for row in range(5))
                totals = [jnp.zeros((block, lanes), wide) for _ in range(16)]
                for pair in range(pairs):
                    column = slice(pair, pair + 1)
                    bottom_real = squares[:, column] * cosine_square - sine_square
                    bottom_imag = decay[:, column] * cross
                    size = 1.0 / (bottom_real * bottom_real + bottom_imag * bottom_imag)
                    part_real = bottom_real * size
                    part_imag = bottom_imag * size
                    for which in range(4):
                        flat, slope = flats[which][:, column], slopes[which][:, column]
                        totals[4 * which] += flat * part_real
                        totals[4 * which + 1] += flat * part_imag
                        totals[4 * which + 2] += slope * part_real
                        totals[4 * which + 3] += slope * part_imag
                sums = [
                    (
                        cosine * totals[4 * which] + sine * totals[4 * which + 3],
                        sine * totals[4 * which + 2] - cosine * totals[4 * which + 1],
                    )
                    for which in range(4)
                ]
                scale = step * cosine
                guard_real = 1.0 + scale * sums[3][0]
                guard_imag = scale * sums[3][1]
                guard_size = scale / (guard_real * guard_real + guard_imag * guard_imag)
                both = complex_product(sums[1], sums[2])
                inner_real = sums[0][0] - (both[0] * guard_real + both[1] * guard_imag) * guard_size
                inner_imag = sums[0][1] - (both[1] * guard_real - both[0] * guard_imag) * guard_size
                khat_real = step * (cosine * inner_real - sine * inner_imag)
                khat_imag = step * (cosine * inner_imag + sine * inner_real)
                if start == 0:
                    first = lax.broadcasted_iota(jnp.int32, (block, lanes), 1) == 0
                    khat_imag = jnp.where(first, last, khat_imag)
                target = pl.ds(at * block, block)
                khat_ref[target, start : start + lanes] = khat_real
                khat_ref[target, half + start : half + start + lanes] = khat_imag
            return 0

        lax.fori_loop(0, share // block, one_block, 0)
        out_ref[...] = split_dot(split(khat_ref[...]), (high_ref[...], rest_ref[...])).astype(low)

    vmem = pl.BlockSpec(memory_space=pltpu.VMEM)
    return pl.pallas_call(
        kernel,
        out_shape=jax.ShapeDtypeStruct((share, row_count), low),
        in_specs=[pl.BlockSpec(memory_space=pltpu.SMEM)] + [vmem] * 9,
        out_specs=vmem,
        scratch_shapes=[pltpu.VMEM((share, row_count), wide), pltpu.VMEM((wide_block, 8), wide)]
        + [pltpu.VMEM((wide_block, pairs), wide)] * 2
        + [pltpu.VMEM((2, wide_block, pairs), wide)] * 3,
        cost_estimate=pl.CostEstimate(flops=1 << 20, transcendentals=0, bytes_accessed=1 << 20),
        compiler_params=kernel_params(),
        name="taps_kernel",
    )(
        dp_place.reshape(1).astype(jnp.int32), jnp.asarray(response_rows(row_count)), *response, step_log[None],
        lam_log_re.T, lam_im.T, *(jnp.swapaxes(values, 1, 2) for values in (p_vec, b_vec, c_vec)),
    )


def place_blocks(every, stride, block, place_rows, block_owner, count, parts=None):
    rows, offsets = place_rows
    width = every.shape[1]
    columns = width * len(offsets)
    part_width = columns // parts if parts else columns
    group = math.gcd(count, 4)
    pieces = [
        (member, offset + step, at, step)
        for member in range(group)
        for at, offset in enumerate(offsets)
        for step in range(0, rows, block)
    ]

    def kernel(*refs):
        out_ref = refs[-1]
        for (member, _, at, step), source in zip(pieces, refs[:-1]):
            target = slice(member * rows + step, member * rows + step + block)
            if parts:
                for part in range(parts):
                    out_ref[target, part, :] = source[:, part * part_width : (part + 1) * part_width].astype(wide)
            else:
                out_ref[target, at * width : (at + 1) * width] = source[...].astype(wide)

    def piece_spec(member, start):
        return pl.BlockSpec(
            (block, width),
            lambda at: (block_owner(at * group + member) * (stride // block) + start // block, 0),
        )

    shape = (parts, part_width) if parts else (columns,)
    return pl.pallas_call(
        kernel,
        out_shape=jax.ShapeDtypeStruct((rows * count,) + shape, wide),
        grid=(count // group,),
        in_specs=[piece_spec(piece[0], piece[1]) for piece in pieces],
        out_specs=pl.BlockSpec((group * rows,) + shape, lambda at: (at,) + (0,) * len(shape)),
        cost_estimate=pl.CostEstimate(flops=0, transcendentals=0, bytes_accessed=rows * count * columns * 6),
        compiler_params=pltpu.CompilerParams(vmem_limit_bytes=32 << 20),
        name="place_blocks",
    )(*([every] * len(pieces)))


def unpack_parameters(packed, pairs):
    width = packed.shape[0]

    def kernel(packed_ref, decay_ref, turn_ref, p_ref, b_ref, c_ref, step_ref):
        columns = packed_ref[...].T

        def piece(at):
            return columns[at * pairs : (at + 1) * pairs]

        decay_ref[...] = piece(0)
        turn_ref[...] = piece(1)
        for at, target in ((2, p_ref), (4, b_ref), (6, c_ref)):
            target[0] = piece(at)
            target[1] = piece(at + 1)
        step_ref[...] = columns[8 * pairs : 8 * pairs + 1]

    flat = jax.ShapeDtypeStruct((pairs, width), wide)
    both = jax.ShapeDtypeStruct((2, pairs, width), wide)
    outs = pl.pallas_call(
        kernel,
        out_shape=(flat, flat, both, both, both, jax.ShapeDtypeStruct((1, width), wide)),
        compiler_params=pltpu.CompilerParams(vmem_limit_bytes=32 << 20),
        name="unpack_parameters",
    )(packed)
    return tuple(jnp.swapaxes(piece, -1, -2) for piece in outs[:5]) + (outs[5],)


def solution(mesh):
    dp = mesh.shape["dp"]
    mp = mesh.shape["mp"]

    def body(
        tokens,
        pack_class,
        ln1_gain,
        ln1_bias,
        step_log,
        lam_log_re,
        lam_im,
        p_vec,
        b_vec,
        c_vec,
        skip,
        glu_weight,
        glu_bias,
        ln2_gain,
        ln2_bias,
        up_weight,
        up_bias,
        down_weight,
        down_bias,
        out_grad,
    ):
        row_count, width = tokens.shape
        features = width * mp
        pairs = lam_log_re.shape[1]
        class_index = pack_class[0]
        mp_place = lax.axis_index("mp")
        dp_place = lax.axis_index("dp")

        swap = [(0, 1), (1, 0)]

        def mp_gather(values):
            if mp != 2:
                return lax.all_gather(values, "mp", axis=1, tiled=True)
            other = lax.ppermute(values, "mp", swap)
            return jnp.where(
                mp_place == 0,
                jnp.concatenate([values, other], axis=1),
                jnp.concatenate([other, values], axis=1),
            )

        def mp_parts(values):
            if mp != 2:
                return (lax.all_gather(values, "mp", axis=1, tiled=True),)
            return (values, lax.ppermute(values, "mp", swap))

        def part_rows(weight):
            if mp != 2:
                return (weight,)
            return (
                lax.dynamic_slice_in_dim(weight, mp_place * width, width, 0),
                lax.dynamic_slice_in_dim(weight, (1 - mp_place) * width, width, 0),
            )

        def part_half(parts, side):
            if mp != 2:
                half = features // 2
                return lax.dynamic_slice_in_dim(parts[0], side * half, half, 1)
            return jnp.where(side == mp_place, parts[0], parts[1])

        def mp_total(values):
            if mp != 2:
                return lax.psum(values, "mp")
            return values + lax.ppermute(values, "mp", swap)

        def mp_scatter_product(left, weight_parts, contract):
            if mp != 2:
                part = lax.dot_general(left, weight_parts[0], contract, preferred_element_type=wide)
                return lax.psum_scatter(part, "mp", scatter_dimension=1, tiled=True)
            sent = lax.dot_general(left, weight_parts[1], contract, preferred_element_type=wide).astype(low)
            arrived = lax.ppermute(sent, "mp", swap)
            return lax.dot_general(left, weight_parts[0], contract, preferred_element_type=wide) + arrived.astype(wide)

        def row_moments(values):
            mean_own = jnp.mean(values, axis=1)
            centred = values - mean_own[:, None]
            return (centred, jnp.stack([mean_own, jnp.sum(centred * centred, axis=1)]))

        def join_moments(own):
            if mp != 2:
                every = lax.all_gather(own, "mp")
                mean_row = jnp.mean(every[:, 0], axis=0)
                gaps = every[:, 0] - mean_row
                var_row = jnp.sum(every[:, 1], axis=0) / features + jnp.mean(gaps * gaps, axis=0)
                return (mean_row, lax.rsqrt(var_row + epsilon), None)
            other = lax.ppermute(own, "mp", swap)
            mean_row = 0.5 * (own[0] + other[0])
            gap = 0.5 * (own[0] - other[0])
            var_row = (own[1] + other[1]) / features + gap * gap
            return (mean_row, lax.rsqrt(var_row + epsilon), other[0])

        def tie(critical, arrays):
            if not arrays:
                return critical
            return lax.optimization_barrier((critical, tuple(arrays)))[0]

        def advance(critical, *sums):
            critical, waited = lax.optimization_barrier((critical, [total.pending for total in sums]))
            sent = []
            for total, arrived in zip(sums, waited):
                total.pending = arrived
                sent.append(total.step())
            return tie(critical, sent)

        def fill(critical, *sums):
            return tie(critical, [total.step() for total in sums])

        def dp_small_total(values):
            if dp & (dp - 1):
                return lax.psum(values, "dp")
            for turn in range(dp.bit_length() - 1):
                values = values + lax.ppermute(values, "dp", swap_pairs(dp, 1 << turn))
            return values

        inputs = tokens.astype(wide)
        near1, moments1 = row_moments(inputs)
        mean1, scale1, _ = join_moments(moments1)
        ln2_both = jnp.stack([ln2_gain, ln2_bias])
        if mp == 2:
            ln2_other = lax.ppermute(ln2_both, "mp", swap)
            ln2_features = jnp.where(
                mp_place == 0,
                jnp.concatenate([ln2_both, ln2_other], axis=1),
                jnp.concatenate([ln2_other, ln2_both], axis=1),
            )
        else:
            ln2_features = lax.all_gather(ln2_both, "mp", axis=1, tiled=True)
        mean1, ln2_features, out_grad = lax.optimization_barrier((mean1, ln2_features, out_grad))
        grad_full = mp_gather(out_grad)
        span = jnp.right_shift(row_count, jnp.where(class_index == 0, 0, class_index + 1))
        inverse_scale = 1.0 / span.astype(wide)
        choice = jnp.stack(
            [jnp.maximum(2 * class_index - 1, 0), 2 * class_index, span, class_index]
        ).astype(jnp.int32)
        tables = transform_tables(row_count)
        tables, turned, table = (
            tuple(jnp.asarray(piece) for piece in tables[:2]),
            tuple(jnp.asarray(piece) for piece in tables[2:4]),
            lax.dynamic_index_in_dim(jnp.asarray(tables[4]), class_index, 0, keepdims=False),
        )
        response = jnp.asarray(response_table(row_count))

        share = width // dp

        def own_share(values, axis):
            return lax.dynamic_slice_in_dim(values, dp_place * share, share, axis)

        shares = (
            own_share(step_log, 0),
            own_share(lam_log_re, 0),
            own_share(lam_im, 0),
            own_share(p_vec, 1),
            own_share(b_vec, 1),
            own_share(c_vec, 1),
        )
        own_shares = shares
        parts = tuple(jnp.asarray(piece) for piece in split_table(response_table(row_count)))
        taps_share = taps_kernel(
            row_count, share, dp_place, parts, step_log, lam_log_re, lam_im, p_vec, b_vec, c_vec
        )
        taps = dp_gather(taps_share, dp)

        centred1 = (near1 + (moments1[0] - mean1)[:, None]) * scale1[:, None]
        normed1 = centred1 * ln1_gain + ln1_bias
        input_spectrum = jnp.dot(table, normed1, precision=lax.Precision.HIGH)
        taps_real, taps_imag, convolved = convolve(choice, tables, turned, input_spectrum, taps)
        taps_spectrum = (taps_real, taps_imag)
        convolved = convolved * inverse_scale
        act, act_slope = gelu_pair(convolved + skip * normed1)
        act_low, grad_full = lax.optimization_barrier((act.astype(low), grad_full))
        grad_out = out_grad.astype(wide)
        down_bias_grad = jnp.sum(grad_out, axis=0)
        glu_flat = glu_weight.reshape(features, 2 * width)
        glu_parts = part_rows(glu_flat)
        up_parts = part_rows(up_weight)
        glu_bias_flat = glu_bias.reshape(2 * width)
        ln2_high = ln2_features.astype(low)
        ln2_rest = (ln2_features - ln2_high.astype(wide)).astype(low)
        up_sums = jnp.dot(jnp.concatenate([ln2_high, ln2_rest]), up_weight, preferred_element_type=wide)
        up_gain_sum = up_sums[0] + up_sums[2]
        up_bias_sum = up_sums[1] + up_sums[3] + up_bias

        act_parts = mp_parts(act_low)
        own_shares = lax.optimization_barrier((own_shares, act_low))[0]
        coefficients, coefficients_back = jax.vjp(channel_coefficients, *own_shares)
        pair_sums = channel_sums(row_count, *coefficients[2:])
        if mp == 2:
            act_far, pair_sums, coefficients = lax.optimization_barrier((act_parts[1], pair_sums, coefficients))
            act_parts = (act_parts[0], act_far)
        proj = glu_bias_flat
        for part, weight in zip(act_parts, glu_parts):
            proj = proj + jnp.dot(part, weight, preferred_element_type=wide)
        value = proj[:, :width]
        gate = jax.nn.sigmoid(proj[:, width:])
        mid = inputs + value * gate

        near2, moments2 = row_moments(mid)
        mean2, scale2, other_mean2 = join_moments(moments2)
        centred2 = (near2 + (moments2[0] - mean2)[:, None]) * scale2[:, None]
        own2 = (centred2 * ln2_gain + ln2_bias).astype(low)
        if mp != 2:
            normed_parts = (lax.all_gather(own2, "mp", axis=1, tiled=True),)
        else:
            other2 = lax.ppermute(tie(near2.astype(low), [mean2]), "mp", swap).astype(wide)
            other2 = (other2 + (other_mean2 - mean2)[:, None]) * scale2[:, None]
            normed_parts = (own2, (other2 * ln2_other[0] + ln2_other[1]).astype(low))

        pre_act = up_bias
        for part, weight in zip(normed_parts, up_parts):
            pre_act = pre_act + jnp.dot(part, weight, preferred_element_type=wide)
        hidden, slope = gelu_pair(pre_act)
        hidden = hidden.astype(low)
        over_columns = (((1,), (1,)), ((), ()))
        over_rows = (((0,), (0,)), ((), ()))
        hidden_grad = lax.dot_general(grad_full, down_weight, over_columns, preferred_element_type=wide)
        pre_wide = hidden_grad * slope
        pre_grad = pre_wide.astype(low)
        row_sums = jnp.stack(
            [jnp.sum(pre_wide * up_gain_sum, axis=1), jnp.sum(pre_wide * (pre_act - up_bias_sum), axis=1)]
        )
        totals2 = mp_total(row_sums) / features
        up_bias_grad = jnp.sum(pre_grad.astype(wide), axis=0)

        def scatter_send(left, parts, contract):
            if mp != 2:
                part = lax.dot_general(left, parts[0], contract, preferred_element_type=wide)
                return (lax.psum_scatter(part, "mp", scatter_dimension=1, tiled=True), ())
            sent = lax.dot_general(left, parts[1], contract, preferred_element_type=wide).astype(low)
            return (lax.ppermute(sent, "mp", swap), sent)

        def scatter_join(left, parts, contract, arrived):
            if mp != 2:
                return arrived
            return lax.dot_general(left, parts[0], contract, preferred_element_type=wide) + arrived.astype(wide)

        def hidden_product(side):
            half = hidden.shape[1] // 2
            return lax.dot_general(
                lax.dynamic_slice_in_dim(hidden, side * half, half, 1), grad_full, over_rows, preferred_element_type=wide
            )

        def up_product(side):
            return lax.dot_general(part_half(normed_parts, side), pre_grad, over_rows, preferred_element_type=wide)

        def glu_product(side):
            return lax.dot_general(part_half(act_parts, side), proj_grad, over_rows, preferred_element_type=wide)

        totals2, pre_sent = lax.optimization_barrier((totals2, pre_grad))
        arrived2, _ = scatter_send(pre_sent, up_parts, over_columns)
        down_sum = WeightSum(hidden_product, dp, dp_place, False)
        up_sum = WeightSum(up_product, dp, dp_place, True)
        arrived2 = fill(arrived2, down_sum, up_sum)
        normed2_grad = scatter_join(pre_grad, up_parts, over_columns, arrived2)
        back2 = scale2[:, None] * (normed2_grad * ln2_gain - totals2[0][:, None] - centred2 * totals2[1][:, None])
        ln2_gain_grad = jnp.sum(normed2_grad * centred2, axis=0)
        ln2_bias_grad = jnp.sum(normed2_grad, axis=0)
        mid_grad = grad_out + back2
        value_grad = mid_grad * gate
        gate_grad = value_grad * value * (1.0 - gate)
        proj_grad = jnp.concatenate([value_grad, gate_grad], axis=1).astype(low)
        proj_grad = advance(proj_grad, down_sum, up_sum)
        glu_bias_grad = jnp.sum(proj_grad.astype(wide), axis=0)
        arrived1, sent1 = scatter_send(proj_grad, glu_parts, over_columns)
        hidden, proj_grad = lax.optimization_barrier((hidden, proj_grad, sent1))[:2]
        glu_sum = WeightSum(glu_product, dp, dp_place, False)
        arrived1 = fill(arrived1, glu_sum)
        if mp == 2:
            down_columns = (
                lax.dynamic_slice_in_dim(down_weight, mp_place * width, width, 1),
                lax.dynamic_slice_in_dim(down_weight, (1 - mp_place) * width, width, 1),
            )
            out_sent = jnp.dot(hidden, down_columns[1], preferred_element_type=wide).astype(low)
            out_own = jnp.dot(hidden, down_columns[0], preferred_element_type=wide) + down_bias + mid
            arrived1 = tie(arrived1, [out_sent, out_own])
        arrived1 = advance(arrived1, down_sum, up_sum, glu_sum)
        act_grad = scatter_join(proj_grad, glu_parts, over_columns, arrived1)
        if mp == 2:
            out_arrived = lax.ppermute(tie(out_sent, [act_grad]), "mp", swap)
        mixed_grad = act_grad * act_slope
        skip_grad = jnp.sum(mixed_grad * normed1, axis=0)
        grad_spectrum = jnp.dot(table, mixed_grad, precision=lax.Precision.HIGH)
        grad_spectrum = advance(grad_spectrum, down_sum, up_sum, glu_sum)
        taps_grad = correlate_taps(choice, tables, grad_spectrum, input_spectrum)
        taps_grad = taps_grad * inverse_scale
        taps_grad = advance(taps_grad, glu_sum)
        shares = [total.finish() for total in (down_sum, up_sum, glu_sum)]
        taps_grad_share, shares = dp_scatter_sum(taps_grad, dp, shares)
        every, stride, block, places = gather_shares(shares, dp)
        khat_grad = lax.dot_general(
            taps_grad_share, response, (((1,), (1,)), ((), ())), precision=lax.Precision.HIGH
        )
        _, response_back = jax.vjp(
            lambda step, last, sums: channel_response(row_count, step, last, sums), *coefficients[:2], pair_sums
        )
        step_part, last_part, sums_part = response_back(khat_grad)
        _, sums_back = jax.vjp(lambda *items: channel_sums(row_count, *items), *coefficients[2:])
        parts = coefficients_back((step_part, last_part) + sums_back(sums_part))
        packed = jnp.concatenate(
            [parts[1], parts[2]]
            + [parts[which][side] for which in (3, 4, 5) for side in (0, 1)]
            + [jnp.broadcast_to(parts[0][:, None], (share, 128))],
            axis=1,
        )
        packed, grad_spectrum = lax.optimization_barrier((packed, grad_spectrum))
        packed = dp_gather(packed, dp)
        normed1_grad = skip * mixed_grad + inverse_scale * correlate_rows(choice, turned, grad_spectrum, taps_spectrum)
        scaled1 = normed1_grad * ln1_gain
        totals1 = mp_total(jnp.stack([jnp.sum(scaled1, axis=1), jnp.sum(scaled1 * centred1, axis=1)])) / features
        totals1, every = lax.optimization_barrier((totals1, every))
        back1 = scale1[:, None] * (scaled1 - totals1[0][:, None] - centred1 * totals1[1][:, None])
        ln1_gain_grad = jnp.sum(normed1_grad * centred1, axis=0)
        ln1_bias_grad = jnp.sum(normed1_grad, axis=0)
        tokens_grad = (mid_grad + back1).astype(low)

        if mp == 2:
            result = (out_own + tie(out_arrived, [totals1]).astype(wide)).astype(low)
        else:
            part = jnp.dot(hidden, down_weight, preferred_element_type=wide)
            result = lax.psum_scatter(part, "mp", scatter_dimension=1, tiled=True)
            result = (result + down_bias + mid).astype(low)
        down_weight_grad = place_blocks(every, stride, block, places[0], down_sum.block_owner, dp)
        up_weight_grad = place_blocks(every, stride, block, places[1], up_sum.block_owner, dp)
        glu_weight_grad = place_blocks(every, stride, block, places[2], glu_sum.block_owner, dp, 2)
        lam_log_re_grad, lam_im_grad, p_grad, b_grad, c_grad, step_grad = unpack_parameters(packed, pairs)
        step_grad = step_grad[0]
        smalls = (
            ln1_gain_grad,
            ln1_bias_grad,
            skip_grad,
            glu_bias_grad,
            ln2_gain_grad,
            ln2_bias_grad,
            up_bias_grad,
            down_bias_grad,
        )
        joined = dp_small_total(jnp.concatenate(smalls).reshape(-1, 128)).reshape(-1)
        split = []
        start = 0
        for small in smalls:
            split.append(joined[start : start + small.shape[0]])
            start += small.shape[0]
        (
            ln1_gain_grad,
            ln1_bias_grad,
            skip_grad,
            glu_bias_grad,
            ln2_gain_grad,
            ln2_bias_grad,
            up_bias_grad,
            down_bias_grad,
        ) = split
        glu_bias_grad = glu_bias_grad.reshape(2, width)
        return (
            result,
            tokens_grad,
            ln1_gain_grad,
            ln1_bias_grad,
            step_grad,
            lam_log_re_grad,
            lam_im_grad,
            p_grad,
            b_grad,
            c_grad,
            skip_grad,
            glu_weight_grad,
            glu_bias_grad,
            ln2_gain_grad,
            ln2_bias_grad,
            up_weight_grad,
            up_bias_grad,
            down_weight_grad,
            down_bias_grad,
        )

    return jax.shard_map(
        body,
        mesh=mesh,
        in_specs=(
            P("dp", "mp"),
            P("dp"),
            P("mp"),
            P("mp"),
            P("mp"),
            P("mp", None),
            P("mp", None),
            P(None, "mp", None),
            P(None, "mp", None),
            P(None, "mp", None),
            P("mp"),
            P(None, None, "mp"),
            P(None, "mp"),
            P("mp"),
            P("mp"),
            P(None, "mp"),
            P("mp"),
            P("mp", None),
            P("mp"),
            P("dp", "mp"),
        ),
        out_specs=(
            P("dp", "mp"),
            P("dp", "mp"),
            P("mp"),
            P("mp"),
            P("mp"),
            P("mp", None),
            P("mp", None),
            P(None, "mp", None),
            P(None, "mp", None),
            P(None, "mp", None),
            P("mp"),
            P(None, None, "mp"),
            P(None, "mp"),
            P("mp"),
            P("mp"),
            P(None, "mp"),
            P("mp"),
            P("mp", None),
            P("mp"),
        ),
        check_vma=False,
    )
```
